32 devices in a mesh: video: 4 (over x, core), tm: 8 (over z, y).
Axes of the slice: x: 2, y: 2, z: 4, core: 2. Of those that a mesh axis runs over, the one named last changes fastest.
Arguments:
- queries: bfloat16 [4, 8, 4096, 256], P('video', 'tm'), may hold values from -720 to 720
- memory: bfloat16 [4, 8, 64, 4096], P('video', 'tm'), may hold values from -6 to 6
- tpos: float32 [7, 64], replicated, may hold values from -4 to 4
- w_k: bfloat16 [64, 256], replicated, may hold values from -0.75 to 0.75
- w_v: bfloat16 [64, 256], replicated, may hold values from -0.75 to 0.75
- w_o: bfloat16 [256, 256], replicated, may hold values from -0.375 to 0.375
- keyframes: int32 [4, 8, 64], P('video', 'tm'), may hold values from 0 to 511, as said below
- cot: bfloat16 [4, 8, 4096, 256], P('video', 'tm'), may hold values from -6 to 6
Outputs:
- branch: bfloat16 [4, 8, 4096, 256], P('video', 'tm')
- grad_wo: float32 [256, 256], P('tm')
The draws below stay inside these ranges and needn't reach their ends.
Inputs may be any that keep to these rules, and one draw needn't show every extreme that they name: `keyframes`: each frame's list is made of runs of 16 consecutive entries that lie in one frame; the runs of one list lie in different frames.
All inputs are finite; a program needn't handle non-finite values.
Results may differ from the reference program's by a relative error of at most 0.012.
The reference program's roundings to bfloat16 on the way count: a program that leaves them out, or rounds other values in their place, can miss the bound.
Values may be sent and summed in bfloat16 or wider, within the bound.
A program may use at most 128 MiB of HBM per device.

```python
import math
import jax
import jax.numpy as jnp
from jax import lax

D = 256
MD = 64
TT = 64
TILES = 64
KF = 64
KSEL = 8
CLASSES = 8
TPF = 4096
FRAMES = 8
VIDEOS = 4
CAP = 16


def draw_queries(key, part):
    shape = (VIDEOS, FRAMES, TPF, D)
    values = 1.5 * jax.random.normal(key, shape, jnp.float32)
    return jnp.clip(values, -9.0, 9.0).astype(jnp.bfloat16)


def draw_keyframes(key, part):
    groups = KF // CAP
    key_hot, key_score, key_tile = jax.random.split(key, 3)
    hot_count = max(1, FRAMES // 8)
    hot_keys = jax.random.split(key_hot, VIDEOS)
    orders = jnp.stack([jax.random.permutation(hot_keys[video_idx], FRAMES) for video_idx in range(VIDEOS)])
    owner_ids = jnp.arange(FRAMES, dtype=jnp.int32)
    hot_flag = jnp.any(owner_ids[None, :, None] == orders[:, None, :hot_count], axis=-1).astype(jnp.int32)
    scores = jax.random.randint(key_score, (VIDEOS, FRAMES, FRAMES), 0, 1024, dtype=jnp.int32)
    scores = scores + 768 * hot_flag[:, None, :]
    distinct = scores * FRAMES + owner_ids[None, None, :]
    chosen = lax.top_k(distinct, groups)[1].astype(jnp.int32)
    owners = jnp.repeat(chosen, CAP, axis=-1)
    tile_pick = jax.random.randint(key_tile, (VIDEOS, FRAMES, KF), 0, TILES, dtype=jnp.int32)
    return (owners * TILES + tile_pick).astype(jnp.int32)


def steps_of(stream_key, extent, cuts, least, largest):
    factor_of = 1.0
    for dim, blocks in cuts:
        draws = jax.random.uniform(jax.random.fold_in(jax.random.fold_in(stream_key, 6), dim), (blocks,), jnp.float32, least / len(cuts), largest / len(cuts))
        factor_of = factor_of * jnp.repeat(jnp.exp(draws), extent[dim] // blocks).reshape((-1,) + (1,) * (len(extent) - 1 - dim))
    return factor_of


def bell_draw(own_key, shape, deviation, limit, cuts=(), held_as=jnp.bfloat16):
    entries = deviation * jax.random.normal(own_key, shape, jnp.float32)
    if cuts:
        entries = entries * steps_of(own_key, shape, cuts, -0.22, 0.18)
    return jnp.clip(entries, -limit, limit).astype(held_as)


def setup_inputs(seed: int = 0) -> dict:
    streams_of = jax.random.split(jax.random.key(seed), 9)
    queries = draw_queries(jax.random.fold_in(streams_of[8], 71), 0)
    memory = bell_draw(streams_of[1], (VIDEOS, FRAMES, TILES, TT * MD), 1.0, 6.0, ((0, 4), (1, 8)))
    tpos = bell_draw(streams_of[2], (7, MD), 1.0, 4.0, (), jnp.float32)
    w_k = bell_draw(streams_of[3], (MD, D), MD ** -0.5, 0.75)
    w_v = bell_draw(streams_of[4], (MD, D), MD ** -0.5, 0.75)
    w_o = bell_draw(streams_of[5], (D, D), D ** -0.5, 0.375)
    keyframes = draw_keyframes(jax.random.fold_in(streams_of[8], 71), 0)
    cot = bell_draw(streams_of[7], (VIDEOS, FRAMES, TPF, D), 1.0, 6.0, ((0, 4), (1, 8)))
    return dict(queries=queries, memory=memory, tpos=tpos, w_k=w_k, w_v=w_v, w_o=w_o, keyframes=keyframes, cot=cot)


def project_pairs(tiles, position, w_pair):
    leading = tiles.shape[:-1]
    mixed = tiles.reshape(leading + (TT, MD)).astype(jnp.float32) + position
    mixed = mixed.astype(jnp.bfloat16)
    kv_pairs = jnp.dot(mixed.reshape(-1, MD), w_pair, preferred_element_type=jnp.float32)
    return kv_pairs.astype(jnp.bfloat16).reshape(leading + (TT, 2 * D))

def attend(query_tiles, recent_pairs, keyed_pairs, valid_back):
    tile_num = query_tiles.shape[0]
    recent = jnp.transpose(recent_pairs, (1, 0, 2, 3))
    kv_pairs = jnp.concatenate([recent, keyed_pairs], axis=1).reshape(tile_num, (6 + KSEL) * TT, 2 * D)
    key_part = kv_pairs[..., :D]
    value_part = kv_pairs[..., D:]
    scores = jnp.einsum('tqd,tkd->tqk', query_tiles.astype(jnp.float32), key_part.astype(jnp.float32))
    scores = scores * (1.0 / math.sqrt(D))
    live_keys = jnp.concatenate([jnp.repeat(valid_back, TT), jnp.ones((KSEL * TT,), dtype=bool)])
    scores = jnp.where(live_keys[None, None, :], scores, -jnp.inf)
    row_max = lax.optimization_barrier(jnp.max(scores, axis=-1, keepdims=True))
    weights = jnp.exp(scores - row_max)
    weights = (weights / lax.optimization_barrier(jnp.sum(weights, axis=-1, keepdims=True))).astype(jnp.bfloat16)
    attended = jnp.einsum('tqk,tkd->tqd', weights.astype(jnp.float32), value_part.astype(jnp.float32))
    return attended.astype(jnp.bfloat16)

def reference(queries, memory, tpos, w_k, w_v, w_o, keyframes, cot):
    w_pair = jnp.concatenate([w_k, w_v], axis=1)
    offsets = jnp.arange(1, 7, dtype=jnp.int32)
    tile_ids = jnp.arange(TILES, dtype=jnp.int32)
    entry_ids = (tile_ids % CLASSES)[:, None] + CLASSES * jnp.arange(KSEL, dtype=jnp.int32)[None, :]

    def one_frame(frame_index):
        video_idx = frame_index // FRAMES
        frame_idx = frame_index % FRAMES
        frames = memory[video_idx]
        back_frame = frame_idx - offsets
        valid_back = back_frame >= 0
        recent_raw = frames[jnp.maximum(back_frame, 0)]
        recent_pairs = project_pairs(recent_raw, tpos[:6][:, None, None, :], w_pair)
        keyed_raw = frames.reshape(FRAMES * TILES, TT * MD)[keyframes[video_idx, frame_idx]]
        keyed_all = project_pairs(keyed_raw, tpos[6], w_pair)
        keyed_pairs = keyed_all[entry_ids]
        query_tiles = queries[video_idx, frame_idx].reshape(TILES, TT, D)
        return attend(query_tiles, recent_pairs, keyed_pairs, valid_back).reshape(TPF, D)
    attended = lax.map(one_frame, jnp.arange(VIDEOS * FRAMES, dtype=jnp.int32))
    flat = attended.reshape(-1, D)
    branch = jnp.dot(flat, w_o, preferred_element_type=jnp.float32).astype(jnp.bfloat16)
    grad_wo = jnp.dot(flat.T, cot.reshape(-1, D), preferred_element_type=jnp.float32)
    grad_wo = grad_wo / math.sqrt(VIDEOS * FRAMES * TPF)
    return (branch.reshape(queries.shape), grad_wo)
```

```python
import functools
import math

import jax
import jax.numpy as jnp
from jax import lax
from jax.experimental import pallas as pl
from jax.experimental.pallas import tpu as pltpu
from jax.sharding import PartitionSpec as P

TT = 64
MD = 64
BACK = 6
CLASSES = 8
LOW = -1e30
LANES = 2 * TT
MESH = pl.DeviceIdType.MESH
DIMS_T = (((1,), (1,)), ((), ()))


def ring_pos(me, n):
    return jnp.where(me % 2 == 1, (me + 1) // 2, (n - me // 2) % n)


def ring_at(pos, n):
    return jnp.where((pos >= 1) & (pos <= n // 2), 2 * pos - 1, (2 * (n - pos)) % (2 * n))


def split_tokens(packed, position):
    mixed = (packed.astype(jnp.float32) + position).astype(jnp.bfloat16)
    first = lax.broadcasted_iota(jnp.int32, mixed.shape, mixed.ndim - 1) < MD
    zero = jnp.zeros_like(mixed)
    return jnp.concatenate(
        [jnp.where(first, mixed, zero), jnp.where(first, zero, mixed)], axis=mixed.ndim - 2
    )


def kernel(
    n, videos, norm, keyed_ref, own_hbm, q_hbm, cot_hbm, tpos_ref, wk_ref, wv_ref, wo_ref,
    branch_hbm, grad_out,
    frames, raw_ref, q_ref, cot_ref, top_ref, sum_ref, acc_ref, att_ref, branch_ref, wk2, wv2,
    pos_ref, grad_ref, terms, parts, mine, sums,
    local_sem, out_sem, send_r, recv_r, send_l, recv_l, send_a, recv_a, send_b, recv_b,
):
    me = lax.axis_index("tm")
    vid = lax.axis_index("video")
    pos = ring_pos(me, n)
    right = ring_at((pos + 1) % n, n)
    left = ring_at((pos + n - 1) % n, n)
    groups, d = q_ref.shape[0], q_ref.shape[-1]
    tiles = groups * CLASSES
    entries = keyed_ref.shape[0] // CLASSES
    far = n // 2
    half = groups // 2
    scale = 1.0 / math.sqrt(d)
    rows = grad_out.shape[0]

    barrier = pltpu.get_barrier_semaphore()
    for other in (right, left):
        pl.semaphore_signal(barrier, inc=1, device_id={"tm": other}, device_id_type=MESH)
    for step in range(1, videos):
        other = (vid + step) % videos
        pl.semaphore_signal(barrier, inc=1, device_id={"video": other}, device_id_type=MESH)
    locals_ = [
        pltpu.make_async_copy(own_hbm, raw_ref, local_sem.at[0]),
        pltpu.make_async_copy(q_hbm, q_ref, local_sem.at[1]),
        pltpu.make_async_copy(cot_hbm, cot_ref, local_sem.at[2]),
    ]
    for copy in locals_:
        copy.start()
    locals_[0].wait()

    def arrange(g, carry):
        frames[me, g] = jnp.swapaxes(raw_ref[g], 0, 1)
        return carry

    lax.fori_loop(0, groups, arrange, 0)
    pl.semaphore_wait(barrier, 2 + videos - 1)

    def hop(step, piece, rightward):
        origin = ring_at((pos + n - step) % n if rightward else (pos + step) % n, n)
        sems = (send_r, recv_r) if rightward else (send_l, recv_l)
        return pltpu.make_async_remote_copy(
            src_ref=frames.at[origin, piece],
            dst_ref=frames.at[origin, piece],
            send_sem=sems[0].at[step, piece],
            recv_sem=sems[1].at[step, piece],
            device_id={"tm": right if rightward else left},
            device_id_type=MESH,
        )

    def every(count, body):
        def step(i, carry):
            body(i)
            return carry

        lax.fori_loop(0, count, step, 0)

    def first_hops(g):
        hop(0, g, True).start()
        hop(0, g, False).start()

    every(groups, first_hops)

    wk = (wk_ref[...].astype(jnp.float32) * scale).astype(jnp.bfloat16)
    wk2[...] = jnp.concatenate([wk, wk], axis=0)
    wv2[...] = jnp.concatenate([wv_ref[...], wv_ref[...]], axis=0)
    pos_ref[...] = jnp.concatenate([tpos_ref[...], tpos_ref[...]], axis=1)
    top_ref[...] = jnp.full_like(top_ref, LOW)
    sum_ref[...] = jnp.zeros_like(sum_ref)
    acc_ref[...] = jnp.zeros_like(acc_ref)
    grad_ref[...] = jnp.zeros_like(grad_ref)
    locals_[1].wait()

    def keys_of(x):
        return jnp.dot(x, wk2[...], preferred_element_type=jnp.float32).astype(jnp.bfloat16)

    def wide_max(s):
        return jnp.broadcast_to(jnp.max(s, axis=1, keepdims=True), (s.shape[0], LANES))

    def recent(distance, g):
        origins = [ring_at((pos + n - distance) % n, n)]
        if distance < far:
            origins.append(ring_at((pos + distance) % n, n))
        xs, bias = [], []
        for origin in origins:
            offset = me - origin
            live = (offset >= 1) & (offset <= BACK)
            row = pos_ref[pl.ds(jnp.clip(offset - 1, 0, BACK - 1), 1), :]
            xs.append(split_tokens(frames[origin, g], row[None]))
            bias.append(jnp.full((1, TT), jnp.where(live, 0.0, LOW), jnp.float32))
        x = jnp.concatenate(xs, axis=1)
        width = x.shape[1]
        bias = jnp.concatenate(bias, axis=1)
        keys = keys_of(x.reshape(CLASSES * width, 2 * MD))
        s = jnp.concatenate(
            [
                lax.dot_general(
                    q_ref[g, c],
                    keys[c * width : (c + 1) * width],
                    DIMS_T,
                    preferred_element_type=jnp.float32,
                )
                for c in range(CLASSES)
            ],
            axis=0,
        )
        s = s + bias
        old = top_ref[g].reshape(CLASSES * TT, LANES)
        top = jnp.maximum(old, wide_max(s))
        p = jnp.exp(s - top[:, :width])
        fade = jnp.exp(old - top)
        part = p if width == LANES else jnp.concatenate([p, jnp.zeros_like(p)], axis=1)
        total = sum_ref[g].reshape(CLASSES * TT, LANES) * fade + part
        p = p.astype(jnp.bfloat16)
        u = jnp.concatenate(
            [
                jnp.dot(p[c * TT : (c + 1) * TT], x[c], preferred_element_type=jnp.float32)
                for c in range(CLASSES)
            ],
            axis=0,
        )
        acc = acc_ref[g].reshape(CLASSES * TT, 2 * MD) * fade + u
        top_ref[g] = top.reshape(CLASSES, TT, LANES)
        sum_ref[g] = total.reshape(CLASSES, TT, LANES)
        acc_ref[g] = acc.reshape(CLASSES, TT, 2 * MD)

    for distance in range(1, far):

        def arrive(g, distance=distance):
            for rightward in (True, False):
                hop(distance - 1, g, rightward).wait_recv()
                if distance < far - 1:
                    hop(distance, g, rightward).start()
            if distance == far - 1:
                @pl.when(g < half)
                def _():
                    hop(distance, g, True).start()

                @pl.when(g >= half)
                def _():
                    hop(distance, g, False).start()

            recent(distance, g)

        every(groups, arrive)

    def last(i):
        hop(far - 1, i, True).wait_recv()
        hop(far - 1, half + i, False).wait_recv()
        recent(far, i)
        recent(far, half + i)

    every(half, last)
    locals_[2].wait()

    def finish(cls, carry):
        top = top_ref[:, cls].reshape(groups * TT, LANES)
        picked = []
        for s in range(entries):
            k = keyed_ref[cls + CLASSES * s]
            picked.append(frames[k // tiles, (k % tiles) // CLASSES, k % CLASSES])
        xk = split_tokens(jnp.concatenate(picked, axis=0), pos_ref[BACK : BACK + 1, :])
        q = q_ref[:, cls].reshape(groups * TT, d)
        sk = lax.dot_general(q, keys_of(xk), DIMS_T, preferred_element_type=jnp.float32)
        slabs = [sk[:, i : i + LANES] for i in range(0, sk.shape[1], LANES)]
        new = jnp.maximum(top, wide_max(functools.reduce(jnp.maximum, slabs)))
        pk = [jnp.exp(slab - new) for slab in slabs]
        fade = jnp.exp(top - new)
        total = sum_ref[:, cls].reshape(groups * TT, LANES)
        total = jnp.sum(total * fade + functools.reduce(jnp.add, pk), axis=1, keepdims=True)
        u = acc_ref[:, cls].reshape(groups * TT, 2 * MD) * fade + jnp.dot(
            jnp.concatenate([p.astype(jnp.bfloat16) for p in pk], axis=1),
            xk,
            preferred_element_type=jnp.float32,
        )
        u = u / total
        attended = jnp.dot(
            u.astype(jnp.bfloat16), wv2[...], preferred_element_type=jnp.float32
        ).astype(jnp.bfloat16)
        att_ref[cls] = attended
        grad_ref[...] += lax.dot_general(
            attended,
            cot_ref[:, cls].reshape(groups * TT, d),
            (((0,), (0,)), ((), ())),
            preferred_element_type=jnp.float32,
        )
        return carry

    lax.fori_loop(0, CLASSES, finish, 0, unroll=2)

    def term(step):
        other = (me + step) % n
        return pltpu.make_async_remote_copy(
            src_ref=terms.at[other],
            dst_ref=parts.at[step - 1],
            send_sem=send_a.at[step - 1],
            recv_sem=recv_a.at[step - 1],
            device_id={"tm": other},
            device_id_type=MESH,
        )

    def share_of(step):
        other = (vid + step) % videos
        return pltpu.make_async_remote_copy(
            src_ref=mine,
            dst_ref=sums.at[vid],
            send_sem=send_b.at[step - 1],
            recv_sem=recv_b.at[step - 1],
            device_id={"video": other},
            device_id_type=MESH,
        )

    terms[...] = grad_ref[...].astype(jnp.bfloat16).reshape(terms.shape)
    for step in range(1, n):
        term(step).start()

    def put(cls):
        return pltpu.make_async_copy(branch_ref.at[cls], branch_hbm.at[:, cls], out_sem.at[cls])

    def project(cls, carry):
        out = jnp.dot(att_ref[cls], wo_ref[...], preferred_element_type=jnp.float32)
        branch_ref[cls] = out.astype(jnp.bfloat16).reshape(groups, TT, d)
        put(cls).start()
        return carry

    lax.fori_loop(0, CLASSES, project, 0)

    total = grad_ref[pl.ds(pl.multiple_of(me * rows, 8), rows), :]
    for step in range(1, n):
        term(step).wait_recv()
        total = total + parts[step - 1].astype(jnp.float32)
    mine[...] = total
    for step in range(1, videos):
        share_of(step).start()
    sums[vid] = total
    for step in range(1, videos):
        share_of(step).wait_recv()
    result = sums[0]
    for other in range(1, videos):
        result = result + sums[other]
    grad_out[...] = result * norm

    for step in range(far - 1):

        def sent(g, step=step):
            hop(step, g, True).wait_send()
            hop(step, g, False).wait_send()

        every(groups, sent)

    def last_sent(i):
        hop(far - 1, i, True).wait_send()
        hop(far - 1, half + i, False).wait_send()

    every(half, last_sent)
    for step in range(1, n):
        term(step).wait_send()
    for step in range(1, videos):
        share_of(step).wait_send()
    for cls in range(CLASSES):
        put(cls).wait()


def per_device(n, videos, queries, memory, tpos, w_k, w_v, w_o, keyframes, cot):
    tiles = memory.shape[2]
    d = queries.shape[-1]
    groups = tiles // CLASSES
    grouped = (groups, CLASSES, TT, d)
    packed = (TT // 2, 2 * MD)
    own = jnp.swapaxes(memory[0, 0].reshape((groups, CLASSES) + packed), 1, 2)
    rows = d // n
    vmem = pl.BlockSpec(memory_space=pltpu.VMEM)
    hbm = pl.BlockSpec(memory_space=pl.ANY)
    dma = pltpu.SemaphoreType.DMA
    f32, bf16 = jnp.float32, jnp.bfloat16
    hops = dma((n // 2, groups))
    norm = 1.0 / math.sqrt(videos * n * tiles * TT)
    branch, grad = pl.pallas_call(
        functools.partial(kernel, n, videos, norm),
        out_shape=(
            jax.ShapeDtypeStruct(grouped, bf16),
            jax.ShapeDtypeStruct((rows, d), f32),
        ),
        in_specs=[
            pl.BlockSpec(memory_space=pltpu.SMEM), hbm, hbm, hbm, vmem, vmem, vmem, vmem,
        ],
        out_specs=(hbm, vmem),
        scratch_shapes=[
            pltpu.VMEM((n, groups, CLASSES) + packed, bf16),
            pltpu.VMEM(own.shape, bf16),
            pltpu.VMEM(grouped, bf16),
            pltpu.VMEM(grouped, bf16),
            pltpu.VMEM((groups, CLASSES, TT, LANES), f32),
            pltpu.VMEM((groups, CLASSES, TT, LANES), f32),
            pltpu.VMEM((groups, CLASSES, TT, 2 * MD), f32),
            pltpu.VMEM((CLASSES, groups * TT, d), bf16),
            pltpu.VMEM((CLASSES, groups, TT, d), bf16),
            pltpu.VMEM((2 * MD, d), bf16),
            pltpu.VMEM((2 * MD, d), bf16),
            pltpu.VMEM((BACK + 1, 2 * MD), f32),
            pltpu.VMEM((d, d), f32),
            pltpu.VMEM((n, rows, d), bf16),
            pltpu.VMEM((n - 1, rows, d), bf16),
            pltpu.VMEM((rows, d), f32),
            pltpu.VMEM((videos, rows, d), f32),
            dma((3,)),
            dma((CLASSES,)),
            hops, hops, hops, hops,
            dma((n - 1,)), dma((n - 1,)),
            dma((videos - 1,)), dma((videos - 1,)),
        ],
        compiler_params=pltpu.CompilerParams(
            collective_id=0, has_side_effects=True, vmem_limit_bytes=60 * 1024 * 1024
        ),
        name="attend",
    )(
        keyframes[0, 0], own, queries[0, 0].reshape(grouped), cot[0, 0].reshape(grouped),
        tpos, w_k, w_v, w_o,
    )
    return branch.reshape(queries.shape), grad


def solution(mesh):
    frame_spec = P("video", "tm", None, None)
    in_specs = (frame_spec, frame_spec, P(), P(), P(), P(), P("video", "tm", None), frame_spec)
    out_specs = (frame_spec, P("tm", None))
    return jax.shard_map(
        functools.partial(per_device, mesh.shape["tm"], mesh.shape["video"]),
        mesh=mesh,
        in_specs=in_specs,
        out_specs=out_specs,
        check_vma=False,
    )
```

```python
import functools
import math

import jax
import jax.numpy as jnp
from jax import lax
from jax.experimental import pallas as pl
from jax.experimental.pallas import tpu as pltpu
from jax.sharding import PartitionSpec as P

TT = 64
MD = 64
BACK = 6
CLASSES = 8
LOW = -1e30
LANES = 2 * TT
MESH = pl.DeviceIdType.MESH
DIMS_T = (((1,), (1,)), ((), ()))


def ring_pos(me, n):
    return jnp.where(me % 2 == 1, (me + 1) // 2, (n - me // 2) % n)


def ring_at(pos, n):
    return jnp.where((pos >= 1) & (pos <= n // 2), 2 * pos - 1, (2 * (n - pos)) % (2 * n))


def split_tokens(packed, position):
    mixed = (packed.astype(jnp.float32) + position).astype(jnp.bfloat16)
    first = lax.broadcasted_iota(jnp.int32, mixed.shape, mixed.ndim - 1) < MD
    zero = jnp.zeros_like(mixed)
    return jnp.concatenate(
        [jnp.where(first, mixed, zero), jnp.where(first, zero, mixed)], axis=mixed.ndim - 2
    )


def kernel(
    n, videos, norm, keyed_hbm, own_hbm, q_hbm, cot_hbm, tpos_hbm, wk_hbm, wv_hbm, wo_hbm,
    branch_hbm, grad_out,
    frames, keyed_ref, tpos_ref, wk_ref, wv_ref, wo_ref, raw_ref, q_ref, cot_ref, top_ref, sum_ref, acc_ref, mean_ref, branch_ref, wk2, wv2,
    pos_ref, outer_ref, grad_ref, terms, parts, mine, sums,
    local_sem, out_sem, send_r, recv_r, send_l, recv_l, send_a, recv_a, send_b, recv_b,
):
    me = lax.axis_index("tm")
    vid = lax.axis_index("video")
    pos = ring_pos(me, n)
    right = ring_at((pos + 1) % n, n)
    left = ring_at((pos + n - 1) % n, n)
    groups, d = q_ref.shape[0], q_ref.shape[-1]
    tiles = groups * CLASSES
    entries = keyed_ref.shape[0] // CLASSES
    far = n // 2
    half = groups // 2
    scale = 1.0 / math.sqrt(d)
    rows = grad_out.shape[0]

    barrier = pltpu.get_barrier_semaphore()
    for other in (right, left):
        pl.semaphore_signal(barrier, inc=1, device_id={"tm": other}, device_id_type=MESH)
    for step in range(1, videos):
        other = (vid + step) % videos
        pl.semaphore_signal(barrier, inc=1, device_id={"video": other}, device_id_type=MESH)
    locals_ = [
        pltpu.make_async_copy(own_hbm, raw_ref, local_sem.at[0]),
        pltpu.make_async_copy(q_hbm, q_ref, local_sem.at[1]),
        pltpu.make_async_copy(keyed_hbm, keyed_ref, local_sem.at[2]),
        pltpu.make_async_copy(tpos_hbm, tpos_ref, local_sem.at[3]),
        pltpu.make_async_copy(wk_hbm, wk_ref, local_sem.at[4]),
        pltpu.make_async_copy(wv_hbm, wv_ref, local_sem.at[5]),
        pltpu.make_async_copy(wo_hbm, wo_ref, local_sem.at[6]),
        pltpu.make_async_copy(cot_hbm, cot_ref, local_sem.at[7]),
    ]
    for copy in locals_:
        copy.start()
    locals_[0].wait()

    def arrange(g, carry):
        frames[me, g] = jnp.swapaxes(raw_ref[g], 0, 1)
        return carry

    lax.fori_loop(0, groups, arrange, 0)
    pl.semaphore_wait(barrier, 2 + videos - 1)

    def hop(step, piece, rightward):
        origin = ring_at((pos + n - step) % n if rightward else (pos + step) % n, n)
        sems = (send_r, recv_r) if rightward else (send_l, recv_l)
        return pltpu.make_async_remote_copy(
            src_ref=frames.at[origin, piece],
            dst_ref=frames.at[origin, piece],
            send_sem=sems[0].at[step, piece],
            recv_sem=sems[1].at[step, piece],
            device_id={"tm": right if rightward else left},
            device_id_type=MESH,
        )

    def every(count, body):
        def step(i, carry):
            body(i)
            return carry

        lax.fori_loop(0, count, step, 0)

    def first_hops(g):
        hop(0, g, True).start()
        hop(0, g, False).start()

    every(groups, first_hops)

    for copy in locals_[2:7]:
        copy.wait()
    wk = (wk_ref[...].astype(jnp.float32) * scale).astype(jnp.bfloat16)
    wk2[...] = jnp.concatenate([wk, wk], axis=0)
    wv2[...] = jnp.concatenate([wv_ref[...], wv_ref[...]], axis=0)
    pos_ref[...] = jnp.concatenate([tpos_ref[...], tpos_ref[...]], axis=1)
    top_ref[...] = jnp.full_like(top_ref, LOW)
    sum_ref[...] = jnp.zeros_like(sum_ref)
    acc_ref[...] = jnp.zeros_like(acc_ref)
    outer_ref[...] = jnp.zeros_like(outer_ref)
    locals_[1].wait()

    def keys_of(x):
        return jnp.dot(x, wk2[...], preferred_element_type=jnp.float32).astype(jnp.bfloat16)

    def wide_max(s):
        return jnp.broadcast_to(jnp.max(s, axis=1, keepdims=True), (s.shape[0], LANES))

    def recent(distance, g):
        origins = [ring_at((pos + n - distance) % n, n)]
        if distance < far:
            origins.append(ring_at((pos + distance) % n, n))
        xs, bias = [], []
        for origin in origins:
            offset = me - origin
            live = (offset >= 1) & (offset <= BACK)
            row = pos_ref[pl.ds(jnp.clip(offset - 1, 0, BACK - 1), 1), :]
            xs.append(split_tokens(frames[origin, g], row[None]))
            bias.append(jnp.full((1, TT), jnp.where(live, 0.0, LOW), jnp.float32))
        x = jnp.concatenate(xs, axis=1)
        width = x.shape[1]
        bias = jnp.concatenate(bias, axis=1)
        keys = keys_of(x.reshape(CLASSES * width, 2 * MD))
        s = jnp.concatenate(
            [
                lax.dot_general(
                    q_ref[g, c],
                    keys[c * width : (c + 1) * width],
                    DIMS_T,
                    preferred_element_type=jnp.float32,
                )
                for c in range(CLASSES)
            ],
            axis=0,
        )
        s = s + bias
        old = top_ref[g].reshape(CLASSES * TT, LANES)
        top = jnp.maximum(old, wide_max(s))
        p = jnp.exp(s - top[:, :width])
        fade = jnp.exp(old - top)
        part = p if width == LANES else jnp.concatenate([p, jnp.zeros_like(p)], axis=1)
        total = sum_ref[g].reshape(CLASSES * TT, LANES) * fade + part
        p = p.astype(jnp.bfloat16)
        u = jnp.concatenate(
            [
                jnp.dot(p[c * TT : (c + 1) * TT], x[c], preferred_element_type=jnp.float32)
                for c in range(CLASSES)
            ],
            axis=0,
        )
        acc = acc_ref[g].reshape(CLASSES * TT, 2 * MD) * fade + u
        top_ref[g] = top.reshape(CLASSES, TT, LANES)
        sum_ref[g] = total.reshape(CLASSES, TT, LANES)
        acc_ref[g] = acc.reshape(CLASSES, TT, 2 * MD)

    for distance in range(1, far):

        def arrive(g, distance=distance):
            for rightward in (True, False):
                hop(distance - 1, g, rightward).wait_recv()
                if distance < far - 1:
                    hop(distance, g, rightward).start()
            if distance == far - 1:
                @pl.when(g < half)
                def _():
                    hop(distance, g, True).start()

                @pl.when(g >= half)
                def _():
                    hop(distance, g, False).start()

            recent(distance, g)

        every(groups, arrive)

    def last(i):
        hop(far - 1, i, True).wait_recv()
        hop(far - 1, half + i, False).wait_recv()
        recent(far, i)
        recent(far, half + i)

    every(half, last)
    locals_[7].wait()

    def finish(cls, carry):
        top = top_ref[:, cls].reshape(groups * TT, LANES)
        picked = []
        for s in range(entries):
            k = keyed_ref[cls + CLASSES * s]
            picked.append(frames[k // tiles, (k % tiles) // CLASSES, k % CLASSES])
        xk = split_tokens(jnp.concatenate(picked, axis=0), pos_ref[BACK : BACK + 1, :])
        q = q_ref[:, cls].reshape(groups * TT, d)
        sk = lax.dot_general(q, keys_of(xk), DIMS_T, preferred_element_type=jnp.float32)
        slabs = [sk[:, i : i + LANES] for i in range(0, sk.shape[1], LANES)]
        new = jnp.maximum(top, wide_max(functools.reduce(jnp.maximum, slabs)))
        pk = [jnp.exp(slab - new) for slab in slabs]
        fade = jnp.exp(top - new)
        total = sum_ref[:, cls].reshape(groups * TT, LANES)
        total = jnp.sum(total * fade + functools.reduce(jnp.add, pk), axis=1, keepdims=True)
        u = acc_ref[:, cls].reshape(groups * TT, 2 * MD) * fade + jnp.dot(
            jnp.concatenate([p.astype(jnp.bfloat16) for p in pk], axis=1),
            xk,
            preferred_element_type=jnp.float32,
        )
        u = (u / total).astype(jnp.bfloat16)
        mean_ref[cls] = u
        outer_ref[...] += lax.dot_general(
            u,
            cot_ref[:, cls].reshape(groups * TT, d),
            (((0,), (0,)), ((), ())),
            preferred_element_type=jnp.float32,
        )
        return carry

    lax.fori_loop(0, CLASSES, finish, 0, unroll=CLASSES)

    def term(step):
        other = (me + step) % n
        return pltpu.make_async_remote_copy(
            src_ref=terms.at[other],
            dst_ref=parts.at[step - 1],
            send_sem=send_a.at[step - 1],
            recv_sem=recv_a.at[step - 1],
            device_id={"tm": other},
            device_id_type=MESH,
        )

    def share_of(step):
        other = (vid + step) % videos
        return pltpu.make_async_remote_copy(
            src_ref=mine,
            dst_ref=sums.at[vid],
            send_sem=send_b.at[step - 1],
            recv_sem=recv_b.at[step - 1],
            device_id={"video": other},
            device_id_type=MESH,
        )

    outer = outer_ref[:MD] + outer_ref[MD:]
    high = outer.astype(jnp.bfloat16)
    low = (outer - high.astype(jnp.float32)).astype(jnp.bfloat16)
    grad_ref[...] = sum(
        lax.dot_general(
            wv_ref[...], half_, (((0,), (0,)), ((), ())), preferred_element_type=jnp.float32
        )
        for half_ in (high, low)
    )
    terms[...] = grad_ref[...].astype(jnp.bfloat16).reshape(terms.shape)
    for step in range(1, n):
        term(step).start()

    def put(cls):
        return pltpu.make_async_copy(branch_ref.at[cls], branch_hbm.at[:, cls], out_sem.at[cls])

    def project(cls, carry):
        attended = jnp.dot(mean_ref[cls], wv2[...], preferred_element_type=jnp.float32)
        out = jnp.dot(
            attended.astype(jnp.bfloat16), wo_ref[...], preferred_element_type=jnp.float32
        )
        branch_ref[cls] = out.astype(jnp.bfloat16).reshape(groups, TT, d)
        put(cls).start()
        return carry

    lax.fori_loop(0, CLASSES, project, 0)

    total = grad_ref[pl.ds(pl.multiple_of(me * rows, 8), rows), :]
    for step in range(1, n):
        term(step).wait_recv()
        total = total + parts[step - 1].astype(jnp.float32)
    mine[...] = total
    for step in range(1, videos):
        share_of(step).start()
    sums[vid] = total
    for step in range(1, videos):
        share_of(step).wait_recv()
    result = sums[0]
    for other in range(1, videos):
        result = result + sums[other]
    grad_out[...] = result * norm

    for step in range(far - 1):

        def sent(g, step=step):
            hop(step, g, True).wait_send()
            hop(step, g, False).wait_send()

        every(groups, sent)

    def last_sent(i):
        hop(far - 1, i, True).wait_send()
        hop(far - 1, half + i, False).wait_send()

    every(half, last_sent)
    for step in range(1, n):
        term(step).wait_send()
    for step in range(1, videos):
        share_of(step).wait_send()
    for cls in range(CLASSES):
        put(cls).wait()


def per_device(n, videos, queries, memory, tpos, w_k, w_v, w_o, keyframes, cot):
    tiles = memory.shape[2]
    d = queries.shape[-1]
    groups = tiles // CLASSES
    grouped = (groups, CLASSES, TT, d)
    packed = (TT // 2, 2 * MD)
    own = jnp.swapaxes(memory[0, 0].reshape((groups, CLASSES) + packed), 1, 2)
    rows = d // n
    vmem = pl.BlockSpec(memory_space=pltpu.VMEM)
    hbm = pl.BlockSpec(memory_space=pl.ANY)
    dma = pltpu.SemaphoreType.DMA
    f32, bf16 = jnp.float32, jnp.bfloat16
    hops = dma((n // 2, groups))
    norm = 1.0 / math.sqrt(videos * n * tiles * TT)
    branch, grad = pl.pallas_call(
        functools.partial(kernel, n, videos, norm),
        out_shape=(
            jax.ShapeDtypeStruct(grouped, bf16),
            jax.ShapeDtypeStruct((rows, d), f32),
        ),
        in_specs=[
            hbm, hbm, hbm, hbm, hbm, hbm, hbm, hbm,
        ],
        out_specs=(hbm, vmem),
        scratch_shapes=[
            pltpu.VMEM((n, groups, CLASSES) + packed, bf16),
            pltpu.SMEM(keyframes.shape[2:], jnp.int32),
            pltpu.VMEM(tpos.shape, f32),
            pltpu.VMEM(w_k.shape, bf16),
            pltpu.VMEM(w_v.shape, bf16),
            pltpu.VMEM(w_o.shape, bf16),
            pltpu.VMEM(own.shape, bf16),
            pltpu.VMEM(grouped, bf16),
            pltpu.VMEM(grouped, bf16),
            pltpu.VMEM((groups, CLASSES, TT, LANES), f32),
            pltpu.VMEM((groups, CLASSES, TT, LANES), f32),
            pltpu.VMEM((groups, CLASSES, TT, 2 * MD), f32),
            pltpu.VMEM((CLASSES, groups * TT, 2 * MD), bf16),
            pltpu.VMEM((CLASSES, groups, TT, d), bf16),
            pltpu.VMEM((2 * MD, d), bf16),
            pltpu.VMEM((2 * MD, d), bf16),
            pltpu.VMEM((BACK + 1, 2 * MD), f32),
            pltpu.VMEM((2 * MD, d), f32),
            pltpu.VMEM((d, d), f32),
            pltpu.VMEM((n, rows, d), bf16),
            pltpu.VMEM((n - 1, rows, d), bf16),
            pltpu.VMEM((rows, d), f32),
            pltpu.VMEM((videos, rows, d), f32),
            dma((8,)),
            dma((CLASSES,)),
            hops, hops, hops, hops,
            dma((n - 1,)), dma((n - 1,)),
            dma((videos - 1,)), dma((videos - 1,)),
        ],
        compiler_params=pltpu.CompilerParams(
            collective_id=0, has_side_effects=True, vmem_limit_bytes=60 * 1024 * 1024
        ),
        name="attend",
    )(
        keyframes[0, 0], own, queries[0, 0].reshape(grouped), cot[0, 0].reshape(grouped),
        tpos, w_k, w_v, w_o,
    )
    return branch.reshape(queries.shape), grad


def solution(mesh):
    frame_spec = P("video", "tm", None, None)
    in_specs = (frame_spec, frame_spec, P(), P(), P(), P(), P("video", "tm", None), frame_spec)
    out_specs = (frame_spec, P("tm", None))
    return jax.shard_map(
        functools.partial(per_device, mesh.shape["tm"], mesh.shape["video"]),
        mesh=mesh,
        in_specs=in_specs,
        out_specs=out_specs,
        check_vma=False,
    )
```

```python
import functools
import math

import jax
import jax.numpy as jnp
from jax import lax
from jax.experimental import pallas as pl
from jax.experimental.pallas import tpu as pltpu
from jax.sharding import PartitionSpec as P

TT = 64
MD = 64
BACK = 6
CLASSES = 8
LOW = -1e30
LANES = 2 * TT
MESH = pl.DeviceIdType.MESH
DIMS_T = (((1,), (1,)), ((), ()))


def ring_pos(me, n):
    return jnp.where(me % 2 == 1, (me + 1) // 2, (n - me // 2) % n)


def ring_at(pos, n):
    return jnp.where((pos >= 1) & (pos <= n // 2), 2 * pos - 1, (2 * (n - pos)) % (2 * n))


def split_tokens(packed, position):
    mixed = (packed.astype(jnp.float32) + position).astype(jnp.bfloat16)
    first = lax.broadcasted_iota(jnp.int32, mixed.shape, mixed.ndim - 1) < MD
    zero = jnp.zeros_like(mixed)
    return jnp.concatenate(
        [jnp.where(first, mixed, zero), jnp.where(first, zero, mixed)], axis=mixed.ndim - 2
    )


def kernel(
    n, videos, norm, keyed_hbm, own_hbm, q_hbm, cot_hbm, tpos_hbm, wk_hbm, wv_hbm, wo_hbm,
    branch_out, grad_out,
    frames, keyed_ref, tpos_ref, wk_ref, wv_ref, wo_ref, raw_ref, q_ref, cot_ref, top_ref, sum_ref, acc_ref, mean_ref, wk2, wv2,
    pos_ref, outer_ref, grad_ref, terms, parts, mine, sums,
    local_sem, send_r, recv_r, send_l, recv_l, send_a, recv_a, send_b, recv_b,
):
    me = lax.axis_index("tm")
    vid = lax.axis_index("video")
    pos = ring_pos(me, n)
    right = ring_at((pos + 1) % n, n)
    left = ring_at((pos + n - 1) % n, n)
    groups, d = q_ref.shape[0], q_ref.shape[-1]
    tiles = groups * CLASSES
    entries = keyed_ref.shape[0] // CLASSES
    far = n // 2
    half = groups // 2
    scale = 1.0 / math.sqrt(d)
    rows = grad_out.shape[0]

    barrier = pltpu.get_barrier_semaphore()
    for other in (right, left):
        pl.semaphore_signal(barrier, inc=1, device_id={"tm": other}, device_id_type=MESH)
    for step in range(1, videos):
        other = (vid + step) % videos
        pl.semaphore_signal(barrier, inc=1, device_id={"video": other}, device_id_type=MESH)
    locals_ = [
        pltpu.make_async_copy(own_hbm, raw_ref, local_sem.at[0]),
        pltpu.make_async_copy(q_hbm, q_ref, local_sem.at[1]),
        pltpu.make_async_copy(keyed_hbm, keyed_ref, local_sem.at[2]),
        pltpu.make_async_copy(tpos_hbm, tpos_ref, local_sem.at[3]),
        pltpu.make_async_copy(wk_hbm, wk_ref, local_sem.at[4]),
        pltpu.make_async_copy(wv_hbm, wv_ref, local_sem.at[5]),
        pltpu.make_async_copy(wo_hbm, wo_ref, local_sem.at[6]),
        pltpu.make_async_copy(cot_hbm, cot_ref, local_sem.at[7]),
    ]
    for copy in locals_:
        copy.start()
    locals_[0].wait()

    def arrange(g, carry):
        frames[me, g] = jnp.swapaxes(raw_ref[g], 0, 1)
        return carry

    lax.fori_loop(0, groups, arrange, 0)
    pl.semaphore_wait(barrier, 2 + videos - 1)

    def hop(step, piece, rightward):
        origin = ring_at((pos + n - step) % n if rightward else (pos + step) % n, n)
        sems = (send_r, recv_r) if rightward else (send_l, recv_l)
        return pltpu.make_async_remote_copy(
            src_ref=frames.at[origin, piece],
            dst_ref=frames.at[origin, piece],
            send_sem=sems[0].at[step, piece],
            recv_sem=sems[1].at[step, piece],
            device_id={"tm": right if rightward else left},
            device_id_type=MESH,
        )

    def every(count, body):
        def step(i, carry):
            body(i)
            return carry

        lax.fori_loop(0, count, step, 0)

    def first_hops(g):
        hop(0, g, True).start()
        hop(0, g, False).start()

    every(groups, first_hops)

    for copy in locals_[2:7]:
        copy.wait()
    wk = (wk_ref[...].astype(jnp.float32) * scale).astype(jnp.bfloat16)
    wk2[...] = jnp.concatenate([wk, wk], axis=0)
    wv2[...] = jnp.concatenate([wv_ref[...], wv_ref[...]], axis=0)
    pos_ref[...] = jnp.concatenate([tpos_ref[...], tpos_ref[...]], axis=1)
    top_ref[...] = jnp.full_like(top_ref, LOW)
    sum_ref[...] = jnp.zeros_like(sum_ref)
    acc_ref[...] = jnp.zeros_like(acc_ref)
    outer_ref[...] = jnp.zeros_like(outer_ref)
    locals_[1].wait()

    def keys_of(x):
        return jnp.dot(x, wk2[...], preferred_element_type=jnp.float32).astype(jnp.bfloat16)

    def wide_max(s):
        return jnp.broadcast_to(jnp.max(s, axis=1, keepdims=True), (s.shape[0], LANES))

    def recent(distance, g):
        origins = [ring_at((pos + n - distance) % n, n)]
        if distance < far:
            origins.append(ring_at((pos + distance) % n, n))
        xs, bias = [], []
        for origin in origins:
            offset = me - origin
            live = (offset >= 1) & (offset <= BACK)
            row = pos_ref[pl.ds(jnp.clip(offset - 1, 0, BACK - 1), 1), :]
            xs.append(split_tokens(frames[origin, g], row[None]))
            bias.append(jnp.full((1, TT), jnp.where(live, 0.0, LOW), jnp.float32))
        x = jnp.concatenate(xs, axis=1)
        width = x.shape[1]
        bias = jnp.concatenate(bias, axis=1)
        keys = keys_of(x.reshape(CLASSES * width, 2 * MD))
        s = jnp.concatenate(
            [
                lax.dot_general(
                    q_ref[g, c],
                    keys[c * width : (c + 1) * width],
                    DIMS_T,
                    preferred_element_type=jnp.float32,
                )
                for c in range(CLASSES)
            ],
            axis=0,
        )
        s = s + bias
        old = top_ref[g].reshape(CLASSES * TT, LANES)
        top = jnp.maximum(old, wide_max(s))
        p = jnp.exp(s - top[:, :width])
        fade = jnp.exp(old - top)
        part = p if width == LANES else jnp.concatenate([p, jnp.zeros_like(p)], axis=1)
        total = sum_ref[g].reshape(CLASSES * TT, LANES) * fade + part
        p = p.astype(jnp.bfloat16)
        u = jnp.concatenate(
            [
                jnp.dot(p[c * TT : (c + 1) * TT], x[c], preferred_element_type=jnp.float32)
                for c in range(CLASSES)
            ],
            axis=0,
        )
        acc = acc_ref[g].reshape(CLASSES * TT, 2 * MD) * fade + u
        top_ref[g] = top.reshape(CLASSES, TT, LANES)
        sum_ref[g] = total.reshape(CLASSES, TT, LANES)
        acc_ref[g] = acc.reshape(CLASSES, TT, 2 * MD)

    for distance in range(1, far):

        def arrive(g, distance=distance):
            for rightward in (True, False):
                hop(distance - 1, g, rightward).wait_recv()
                if distance < far - 1:
                    hop(distance, g, rightward).start()
            if distance == far - 1:
                @pl.when(g < half)
                def _():
                    hop(distance, g, True).start()

                @pl.when(g >= half)
                def _():
                    hop(distance, g, False).start()

            recent(distance, g)

        every(groups, arrive)

    def last(i):
        hop(far - 1, i, True).wait_recv()
        hop(far - 1, half + i, False).wait_recv()
        recent(far, i)
        recent(far, half + i)

    every(half, last)
    locals_[7].wait()

    def finish(cls, carry):
        top = top_ref[:, cls].reshape(groups * TT, LANES)
        picked = []
        for s in range(entries):
            k = keyed_ref[cls + CLASSES * s]
            picked.append(frames[k // tiles, (k % tiles) // CLASSES, k % CLASSES])
        xk = split_tokens(jnp.concatenate(picked, axis=0), pos_ref[BACK : BACK + 1, :])
        q = q_ref[:, cls].reshape(groups * TT, d)
        sk = lax.dot_general(q, keys_of(xk), DIMS_T, preferred_element_type=jnp.float32)
        slabs = [sk[:, i : i + LANES] for i in range(0, sk.shape[1], LANES)]
        new = jnp.maximum(top, wide_max(functools.reduce(jnp.maximum, slabs)))
        pk = [jnp.exp(slab - new) for slab in slabs]
        fade = jnp.exp(top - new)
        total = sum_ref[:, cls].reshape(groups * TT, LANES)
        total = jnp.sum(total * fade + functools.reduce(jnp.add, pk), axis=1, keepdims=True)
        u = acc_ref[:, cls].reshape(groups * TT, 2 * MD) * fade + jnp.dot(
            jnp.concatenate([p.astype(jnp.bfloat16) for p in pk], axis=1),
            xk,
            preferred_element_type=jnp.float32,
        )
        u = (u / total).astype(jnp.bfloat16)
        mean_ref[cls] = u
        outer_ref[...] += lax.dot_general(
            u,
            cot_ref[:, cls].reshape(groups * TT, d),
            (((0,), (0,)), ((), ())),
            preferred_element_type=jnp.float32,
        )
        return carry

    lax.fori_loop(0, CLASSES, finish, 0, unroll=CLASSES)

    def term(step):
        other = (me + step) % n
        return pltpu.make_async_remote_copy(
            src_ref=terms.at[other],
            dst_ref=parts.at[step - 1],
            send_sem=send_a.at[step - 1],
            recv_sem=recv_a.at[step - 1],
            device_id={"tm": other},
            device_id_type=MESH,
        )

    def share_of(step):
        other = (vid + step) % videos
        return pltpu.make_async_remote_copy(
            src_ref=mine,
            dst_ref=sums.at[vid],
            send_sem=send_b.at[step - 1],
            recv_sem=recv_b.at[step - 1],
            device_id={"video": other},
            device_id_type=MESH,
        )

    outer = outer_ref[:MD] + outer_ref[MD:]
    high = outer.astype(jnp.bfloat16)
    low = (outer - high.astype(jnp.float32)).astype(jnp.bfloat16)
    grad_ref[...] = sum(
        lax.dot_general(
            wv_ref[...], half_, (((0,), (0,)), ((), ())), preferred_element_type=jnp.float32
        )
        for half_ in (high, low)
    )
    terms[...] = grad_ref[...].astype(jnp.bfloat16).reshape(terms.shape)
    for step in range(1, n):
        term(step).start()

    def project(cls, carry):
        attended = jnp.dot(mean_ref[cls], wv2[...], preferred_element_type=jnp.float32)
        out = jnp.dot(
            attended.astype(jnp.bfloat16), wo_ref[...], preferred_element_type=jnp.float32
        )
        branch_out[:, cls] = out.astype(jnp.bfloat16).reshape(groups, TT, d)
        return carry

    lax.fori_loop(0, CLASSES, project, 0)

    total = grad_ref[pl.ds(pl.multiple_of(me * rows, 8), rows), :]
    for step in range(1, n):
        term(step).wait_recv()
        total = total + parts[step - 1].astype(jnp.float32)
    mine[...] = total
    for step in range(1, videos):
        share_of(step).start()
    sums[vid] = total
    for step in range(1, videos):
        share_of(step).wait_recv()
    result = sums[0]
    for other in range(1, videos):
        result = result + sums[other]
    grad_out[...] = result * norm

    for step in range(far - 1):

        def sent(g, step=step):
            hop(step, g, True).wait_send()
            hop(step, g, False).wait_send()

        every(groups, sent)

    def last_sent(i):
        hop(far - 1, i, True).wait_send()
        hop(far - 1, half + i, False).wait_send()

    every(half, last_sent)
    for step in range(1, n):
        term(step).wait_send()
    for step in range(1, videos):
        share_of(step).wait_send()


def per_device(n, videos, queries, memory, tpos, w_k, w_v, w_o, keyframes, cot):
    tiles = memory.shape[2]
    d = queries.shape[-1]
    groups = tiles // CLASSES
    grouped = (groups, CLASSES, TT, d)
    packed = (TT // 2, 2 * MD)
    own = jnp.swapaxes(memory[0, 0].reshape((groups, CLASSES) + packed), 1, 2)
    rows = d // n
    vmem = pl.BlockSpec(memory_space=pltpu.VMEM)
    hbm = pl.BlockSpec(memory_space=pl.ANY)
    dma = pltpu.SemaphoreType.DMA
    f32, bf16 = jnp.float32, jnp.bfloat16
    hops = dma((n // 2, groups))
    norm = 1.0 / math.sqrt(videos * n * tiles * TT)
    branch, grad = pl.pallas_call(
        functools.partial(kernel, n, videos, norm),
        out_shape=(
            pltpu.VMEM(grouped, bf16),
            pltpu.VMEM((rows, d), f32),
        ),
        in_specs=[
            hbm, hbm, hbm, hbm, hbm, hbm, hbm, hbm,
        ],
        out_specs=(vmem, vmem),
        scratch_shapes=[
            pltpu.VMEM((n, groups, CLASSES) + packed, bf16),
            pltpu.SMEM(keyframes.shape[2:], jnp.int32),
            pltpu.VMEM(tpos.shape, f32),
            pltpu.VMEM(w_k.shape, bf16),
            pltpu.VMEM(w_v.shape, bf16),
            pltpu.VMEM(w_o.shape, bf16),
            pltpu.VMEM(own.shape, bf16),
            pltpu.VMEM(grouped, bf16),
            pltpu.VMEM(grouped, bf16),
            pltpu.VMEM((groups, CLASSES, TT, LANES), f32),
            pltpu.VMEM((groups, CLASSES, TT, LANES), f32),
            pltpu.VMEM((groups, CLASSES, TT, 2 * MD), f32),
            pltpu.VMEM((CLASSES, groups * TT, 2 * MD), bf16),
            pltpu.VMEM((2 * MD, d), bf16),
            pltpu.VMEM((2 * MD, d), bf16),
            pltpu.VMEM((BACK + 1, 2 * MD), f32),
            pltpu.VMEM((2 * MD, d), f32),
            pltpu.VMEM((d, d), f32),
            pltpu.VMEM((n, rows, d), bf16),
            pltpu.VMEM((n - 1, rows, d), bf16),
            pltpu.VMEM((rows, d), f32),
            pltpu.VMEM((videos, rows, d), f32),
            dma((8,)),
            hops, hops, hops, hops,
            dma((n - 1,)), dma((n - 1,)),
            dma((videos - 1,)), dma((videos - 1,)),
        ],
        compiler_params=pltpu.CompilerParams(
            collective_id=0, has_side_effects=True, vmem_limit_bytes=58 * 1024 * 1024
        ),
        name="attend",
    )(
        keyframes[0, 0], own, queries[0, 0].reshape(grouped), cot[0, 0].reshape(grouped),
        tpos, w_k, w_v, w_o,
    )
    return branch.reshape(queries.shape), grad


def solution(mesh):
    frame_spec = P("video", "tm", None, None)
    in_specs = (frame_spec, frame_spec, P(), P(), P(), P(), P("video", "tm", None), frame_spec)
    out_specs = (frame_spec, P("tm", None))
    return jax.shard_map(
        functools.partial(per_device, mesh.shape["tm"], mesh.shape["video"]),
        mesh=mesh,
        in_specs=in_specs,
        out_specs=out_specs,
        check_vma=False,
    )
```

```python
import functools
import math

import jax
import jax.numpy as jnp
from jax import lax
from jax.experimental import pallas as pl
from jax.experimental.pallas import tpu as pltpu
from jax.sharding import PartitionSpec as P

TT = 64
MD = 64
BACK = 6
CLASSES = 8
LOW = -1e30
LANES = 2 * TT
MESH = pl.DeviceIdType.MESH
DIMS_T = (((1,), (1,)), ((), ()))


def ring_pos(me, n):
    return jnp.where(me % 2 == 1, (me + 1) // 2, (n - me // 2) % n)


def ring_at(pos, n):
    return jnp.where((pos >= 1) & (pos <= n // 2), 2 * pos - 1, (2 * (n - pos)) % (2 * n))


def split_tokens(packed, position):
    mixed = (packed.astype(jnp.float32) + position).astype(jnp.bfloat16)
    first = lax.broadcasted_iota(jnp.int32, mixed.shape, mixed.ndim - 1) < MD
    zero = jnp.zeros_like(mixed)
    return jnp.concatenate(
        [jnp.where(first, mixed, zero), jnp.where(first, zero, mixed)], axis=mixed.ndim - 2
    )


def kernel(
    n, videos, norm, keyed_hbm, own_hbm, q_hbm, cot_hbm, tpos_hbm, wk_hbm, wv_hbm, wo_hbm,
    branch_out, grad_out,
    frames, keyed_ref, tpos_ref, wk_ref, wv_ref, wo_ref, raw_ref, q_ref, cot_ref, top_ref, sum_ref, acc_ref, mean_ref, wk2, wv2,
    pos_ref, outer_ref, grad_ref, terms, parts, mine, sums,
    local_sem, send_r, recv_r, send_l, recv_l, send_a, recv_a, send_b, recv_b,
):
    me = lax.axis_index("tm")
    vid = lax.axis_index("video")
    pos = ring_pos(me, n)
    right = ring_at((pos + 1) % n, n)
    left = ring_at((pos + n - 1) % n, n)
    groups, d = q_ref.shape[0], q_ref.shape[-1]
    tiles = groups * CLASSES
    entries = keyed_ref.shape[0] // CLASSES
    far = n // 2
    half = groups // 2
    scale = 1.0 / math.sqrt(d)
    rows = grad_out.shape[0]

    barrier = pltpu.get_barrier_semaphore()
    for other in (right, left):
        pl.semaphore_signal(barrier, inc=1, device_id={"tm": other}, device_id_type=MESH)
    for step in range(1, videos):
        other = (vid + step) % videos
        pl.semaphore_signal(barrier, inc=1, device_id={"video": other}, device_id_type=MESH)
    locals_ = [
        pltpu.make_async_copy(own_hbm, raw_ref, local_sem.at[0]),
        pltpu.make_async_copy(q_hbm, q_ref, local_sem.at[1]),
        pltpu.make_async_copy(keyed_hbm, keyed_ref, local_sem.at[2]),
        pltpu.make_async_copy(tpos_hbm, tpos_ref, local_sem.at[3]),
        pltpu.make_async_copy(wk_hbm, wk_ref, local_sem.at[4]),
        pltpu.make_async_copy(wv_hbm, wv_ref, local_sem.at[5]),
        pltpu.make_async_copy(wo_hbm, wo_ref, local_sem.at[6]),
        pltpu.make_async_copy(cot_hbm, cot_ref, local_sem.at[7]),
    ]
    for copy in locals_:
        copy.start()
    locals_[0].wait()

    def arrange(g, carry):
        frames[me, g] = jnp.swapaxes(raw_ref[g], 0, 1)
        return carry

    lax.fori_loop(0, groups, arrange, 0)
    pl.semaphore_wait(barrier, 2 + videos - 1)

    def hop(step, piece, rightward):
        origin = ring_at((pos + n - step) % n if rightward else (pos + step) % n, n)
        sems = (send_r, recv_r) if rightward else (send_l, recv_l)
        return pltpu.make_async_remote_copy(
            src_ref=frames.at[origin, piece],
            dst_ref=frames.at[origin, piece],
            send_sem=sems[0].at[step, piece],
            recv_sem=sems[1].at[step, piece],
            device_id={"tm": right if rightward else left},
            device_id_type=MESH,
        )

    def every(count, body):
        def step(i, carry):
            body(i)
            return carry

        lax.fori_loop(0, count, step, 0)

    def first_hops(g):
        hop(0, g, True).start()
        hop(0, g, False).start()

    every(groups, first_hops)

    for copy in locals_[2:7]:
        copy.wait()
    wk = (wk_ref[...].astype(jnp.float32) * scale).astype(jnp.bfloat16)
    wk2[...] = jnp.concatenate([wk, wk], axis=0)
    wv2[...] = jnp.concatenate([wv_ref[...], wv_ref[...]], axis=0)
    pos_ref[...] = jnp.concatenate([tpos_ref[...], tpos_ref[...]], axis=1)
    top_ref[...] = jnp.full_like(top_ref, LOW)
    sum_ref[...] = jnp.zeros_like(sum_ref)
    acc_ref[...] = jnp.zeros_like(acc_ref)
    outer_ref[...] = jnp.zeros_like(outer_ref)
    locals_[1].wait()

    def keys_of(x):
        return jnp.dot(x, wk2[...], preferred_element_type=jnp.float32).astype(jnp.bfloat16)

    def wide_max(s):
        return jnp.broadcast_to(jnp.max(s, axis=1, keepdims=True), (s.shape[0], LANES))

    def recent(distance, g):
        origins = [ring_at((pos + n - distance) % n, n)]
        if distance < far:
            origins.append(ring_at((pos + distance) % n, n))
        xs, bias = [], []
        for origin in origins:
            offset = me - origin
            live = (offset >= 1) & (offset <= BACK)
            row = pos_ref[pl.ds(jnp.clip(offset - 1, 0, BACK - 1), 1), :]
            xs.append(split_tokens(frames[origin, g], row[None]))
            bias.append(jnp.full((1, TT), jnp.where(live, 0.0, LOW), jnp.float32))
        x = jnp.concatenate(xs, axis=1)
        width = x.shape[1]
        bias = jnp.concatenate(bias, axis=1)
        keys = keys_of(x.reshape(CLASSES * width, 2 * MD))
        s = jnp.concatenate(
            [
                lax.dot_general(
                    q_ref[g, c],
                    keys[c * width : (c + 1) * width],
                    DIMS_T,
                    preferred_element_type=jnp.float32,
                )
                for c in range(CLASSES)
            ],
            axis=0,
        )
        s = s + bias
        old = top_ref[g].reshape(CLASSES * TT, LANES)
        top = jnp.maximum(old, wide_max(s))
        p = jnp.exp(s - top[:, :width])
        fade = jnp.exp(old - top)
        part = p if width == LANES else jnp.concatenate([p, jnp.zeros_like(p)], axis=1)
        total = sum_ref[g].reshape(CLASSES * TT, LANES) * fade + part
        p = p.astype(jnp.bfloat16)
        u = jnp.concatenate(
            [
                jnp.dot(p[c * TT : (c + 1) * TT], x[c], preferred_element_type=jnp.float32)
                for c in range(CLASSES)
            ],
            axis=0,
        )
        acc = acc_ref[g].reshape(CLASSES * TT, 2 * MD) * fade + u
        top_ref[g] = top.reshape(CLASSES, TT, LANES)
        sum_ref[g] = total.reshape(CLASSES, TT, LANES)
        acc_ref[g] = acc.reshape(CLASSES, TT, 2 * MD)

    for distance in range(1, far):

        def arrive(g, distance=distance):
            for rightward in (True, False):
                hop(distance - 1, g, rightward).wait_recv()
                if distance < far - 1:
                    hop(distance, g, rightward).start()
            if distance == far - 1:
                @pl.when(g < half)
                def _():
                    hop(distance, g, True).start()

                @pl.when(g >= half)
                def _():
                    hop(distance, g, False).start()

            recent(distance, g)

        every(groups, arrive)

    def last(i):
        hop(far - 1, i, True).wait_recv()
        hop(far - 1, half + i, False).wait_recv()
        recent(far, i)
        recent(far, half + i)

    every(half, last)
    locals_[7].wait()

    def finish(cls, carry):
        top = top_ref[:, cls].reshape(groups * TT, LANES)
        picked = []
        for s in range(entries):
            k = keyed_ref[cls + CLASSES * s]
            picked.append(frames[k // tiles, (k % tiles) // CLASSES, k % CLASSES])
        xk = split_tokens(jnp.concatenate(picked, axis=0), pos_ref[BACK : BACK + 1, :])
        q = q_ref[:, cls].reshape(groups * TT, d)
        sk = lax.dot_general(q, keys_of(xk), DIMS_T, preferred_element_type=jnp.float32)
        slabs = [sk[:, i : i + LANES] for i in range(0, sk.shape[1], LANES)]
        new = jnp.maximum(top, wide_max(functools.reduce(jnp.maximum, slabs)))
        pk = [jnp.exp(slab - new) for slab in slabs]
        fade = jnp.exp(top - new)
        total = sum_ref[:, cls].reshape(groups * TT, LANES)
        total = jnp.sum(total * fade + functools.reduce(jnp.add, pk), axis=1, keepdims=True)
        u = acc_ref[:, cls].reshape(groups * TT, 2 * MD) * fade + jnp.dot(
            jnp.concatenate([p.astype(jnp.bfloat16) for p in pk], axis=1),
            xk,
            preferred_element_type=jnp.float32,
        )
        u = (u / total).astype(jnp.bfloat16)
        mean_ref[cls] = u
        outer_ref[...] += lax.dot_general(
            u,
            cot_ref[:, cls].reshape(groups * TT, d),
            (((0,), (0,)), ((), ())),
            preferred_element_type=jnp.float32,
        )
        return carry

    lax.fori_loop(0, CLASSES, finish, 0, unroll=CLASSES)

    def term(step):
        other = (me + step) % n
        return pltpu.make_async_remote_copy(
            src_ref=terms.at[other],
            dst_ref=parts.at[step - 1],
            send_sem=send_a.at[step - 1],
            recv_sem=recv_a.at[step - 1],
            device_id={"tm": other},
            device_id_type=MESH,
        )

    def share_of(step):
        other = (vid + step) % videos
        return pltpu.make_async_remote_copy(
            src_ref=mine,
            dst_ref=sums.at[vid],
            send_sem=send_b.at[step - 1],
            recv_sem=recv_b.at[step - 1],
            device_id={"video": other},
            device_id_type=MESH,
        )

    outer = outer_ref[:MD] + outer_ref[MD:]
    high = outer.astype(jnp.bfloat16)
    low = (outer - high.astype(jnp.float32)).astype(jnp.bfloat16)
    grad_ref[...] = sum(
        lax.dot_general(
            wv_ref[...], half_, (((0,), (0,)), ((), ())), preferred_element_type=jnp.float32
        )
        for half_ in (high, low)
    )
    terms[...] = grad_ref[...].astype(jnp.bfloat16).reshape(terms.shape)
    for step in range(1, n):
        term(step).start()

    def project(cls, carry):
        attended = jnp.dot(mean_ref[cls], wv2[...], preferred_element_type=jnp.float32)
        out = jnp.dot(
            attended.astype(jnp.bfloat16), wo_ref[...], preferred_element_type=jnp.float32
        )
        branch_out[:, cls] = out.astype(jnp.bfloat16).reshape(groups, TT, d)
        return carry

    lax.fori_loop(0, CLASSES, project, 0)

    total = grad_ref[pl.ds(pl.multiple_of(me * rows, 8), rows), :]
    for step in range(1, n):
        term(step).wait_recv()
        total = total + parts[step - 1].astype(jnp.float32)
    total = total.astype(jnp.bfloat16)
    mine[...] = total
    for step in range(1, videos):
        share_of(step).start()
    sums[vid] = total
    for step in range(1, videos):
        share_of(step).wait_recv()
    result = sums[0].astype(jnp.float32)
    for other in range(1, videos):
        result = result + sums[other].astype(jnp.float32)
    grad_out[...] = result * norm

    for step in range(far - 1):

        def sent(g, step=step):
            hop(step, g, True).wait_send()
            hop(step, g, False).wait_send()

        every(groups, sent)

    def last_sent(i):
        hop(far - 1, i, True).wait_send()
        hop(far - 1, half + i, False).wait_send()

    every(half, last_sent)
    for step in range(1, n):
        term(step).wait_send()
    for step in range(1, videos):
        share_of(step).wait_send()


def per_device(n, videos, queries, memory, tpos, w_k, w_v, w_o, keyframes, cot):
    tiles = memory.shape[2]
    d = queries.shape[-1]
    groups = tiles // CLASSES
    grouped = (groups, CLASSES, TT, d)
    packed = (TT // 2, 2 * MD)
    own = jnp.swapaxes(memory[0, 0].reshape((groups, CLASSES) + packed), 1, 2)
    rows = d // n
    vmem = pl.BlockSpec(memory_space=pltpu.VMEM)
    hbm = pl.BlockSpec(memory_space=pl.ANY)
    dma = pltpu.SemaphoreType.DMA
    f32, bf16 = jnp.float32, jnp.bfloat16
    hops = dma((n // 2, groups))
    norm = 1.0 / math.sqrt(videos * n * tiles * TT)
    branch, grad = pl.pallas_call(
        functools.partial(kernel, n, videos, norm),
        out_shape=(
            pltpu.VMEM(grouped, bf16),
            pltpu.VMEM((rows, d), f32),
        ),
        in_specs=[
            hbm, hbm, hbm, hbm, hbm, hbm, hbm, hbm,
        ],
        out_specs=(vmem, vmem),
        scratch_shapes=[
            pltpu.VMEM((n, groups, CLASSES) + packed, bf16),
            pltpu.SMEM(keyframes.shape[2:], jnp.int32),
            pltpu.VMEM(tpos.shape, f32),
            pltpu.VMEM(w_k.shape, bf16),
            pltpu.VMEM(w_v.shape, bf16),
            pltpu.VMEM(w_o.shape, bf16),
            pltpu.VMEM(own.shape, bf16),
            pltpu.VMEM(grouped, bf16),
            pltpu.VMEM(grouped, bf16),
            pltpu.VMEM((groups, CLASSES, TT, LANES), f32),
            pltpu.VMEM((groups, CLASSES, TT, LANES), f32),
            pltpu.VMEM((groups, CLASSES, TT, 2 * MD), f32),
            pltpu.VMEM((CLASSES, groups * TT, 2 * MD), bf16),
            pltpu.VMEM((2 * MD, d), bf16),
            pltpu.VMEM((2 * MD, d), bf16),
            pltpu.VMEM((BACK + 1, 2 * MD), f32),
            pltpu.VMEM((2 * MD, d), f32),
            pltpu.VMEM((d, d), f32),
            pltpu.VMEM((n, rows, d), bf16),
            pltpu.VMEM((n - 1, rows, d), bf16),
            pltpu.VMEM((rows, d), bf16),
            pltpu.VMEM((videos, rows, d), bf16),
            dma((8,)),
            hops, hops, hops, hops,
            dma((n - 1,)), dma((n - 1,)),
            dma((videos - 1,)), dma((videos - 1,)),
        ],
        compiler_params=pltpu.CompilerParams(
            collective_id=0, has_side_effects=True, vmem_limit_bytes=58 * 1024 * 1024
        ),
        name="attend",
    )(
        keyframes[0, 0], own, queries[0, 0].reshape(grouped), cot[0, 0].reshape(grouped),
        tpos, w_k, w_v, w_o,
    )
    return branch.reshape(queries.shape), grad


def solution(mesh):
    frame_spec = P("video", "tm", None, None)
    in_specs = (frame_spec, frame_spec, P(), P(), P(), P(), P("video", "tm", None), frame_spec)
    out_specs = (frame_spec, P("tm", None))
    return jax.shard_map(
        functools.partial(per_device, mesh.shape["tm"], mesh.shape["video"]),
        mesh=mesh,
        in_specs=in_specs,
        out_specs=out_specs,
        check_vma=False,
    )
```

```python
import functools
import math

import jax
import jax.numpy as jnp
from jax import lax
from jax.experimental import pallas as pl
from jax.experimental.pallas import tpu as pltpu
from jax.sharding import PartitionSpec as P

TT = 64
MD = 64
BACK = 6
CLASSES = 8
LOW = -1e30
LANES = 2 * TT
MESH = pl.DeviceIdType.MESH
DIMS_T = (((1,), (1,)), ((), ()))


def ring_pos(me, n):
    return jnp.where(me % 2 == 1, (me + 1) // 2, (n - me // 2) % n)


def ring_at(pos, n):
    return jnp.where((pos >= 1) & (pos <= n // 2), 2 * pos - 1, (2 * (n - pos)) % (2 * n))


def split_tokens(packed, position):
    mixed = (packed.astype(jnp.float32) + position).astype(jnp.bfloat16)
    first = lax.broadcasted_iota(jnp.int32, mixed.shape, mixed.ndim - 1) < MD
    zero = jnp.zeros_like(mixed)
    return jnp.concatenate(
        [jnp.where(first, mixed, zero), jnp.where(first, zero, mixed)], axis=mixed.ndim - 2
    )


def kernel(
    n, videos, norm, keyed_hbm, own_hbm, q_hbm, cot_hbm, tpos_hbm, wk_hbm, wv_hbm, wo_hbm,
    branch_out, grad_out,
    frames, keyed_ref, tpos_ref, wk_ref, wv_ref, wo_ref, raw_ref, q_ref, cot_ref, top_ref, sum_ref, acc_ref, mean_ref, wk2, wv2,
    pos_ref, outer_ref, grad_ref, terms, parts, mine, sums,
    local_sem, send_r, recv_r, send_l, recv_l, send_a, recv_a, send_b, recv_b,
):
    me = lax.axis_index("tm")
    vid = lax.axis_index("video")
    pos = ring_pos(me, n)
    right = ring_at((pos + 1) % n, n)
    left = ring_at((pos + n - 1) % n, n)
    groups, d = q_ref.shape[0], q_ref.shape[-1]
    tiles = groups * CLASSES
    entries = keyed_ref.shape[0] // CLASSES
    far = n // 2
    half = groups // 2
    scale = 1.0 / math.sqrt(d)
    rows = grad_out.shape[0]

    barrier = pltpu.get_barrier_semaphore()
    for other in (right, left):
        pl.semaphore_signal(barrier, inc=1, device_id={"tm": other}, device_id_type=MESH)
    for step in range(1, videos):
        other = (vid + step) % videos
        pl.semaphore_signal(barrier, inc=1, device_id={"video": other}, device_id_type=MESH)
    locals_ = [
        pltpu.make_async_copy(own_hbm, raw_ref, local_sem.at[0]),
        pltpu.make_async_copy(q_hbm, q_ref, local_sem.at[1]),
        pltpu.make_async_copy(keyed_hbm, keyed_ref, local_sem.at[2]),
        pltpu.make_async_copy(tpos_hbm, tpos_ref, local_sem.at[3]),
        pltpu.make_async_copy(wk_hbm, wk_ref, local_sem.at[4]),
        pltpu.make_async_copy(wv_hbm, wv_ref, local_sem.at[5]),
        pltpu.make_async_copy(wo_hbm, wo_ref, local_sem.at[6]),
        pltpu.make_async_copy(cot_hbm, cot_ref, local_sem.at[7]),
    ]
    for copy in locals_:
        copy.start()
    locals_[0].wait()

    def arrange(g, carry):
        frames[me, g] = jnp.swapaxes(raw_ref[g], 0, 1)
        return carry

    lax.fori_loop(0, groups, arrange, 0)
    pl.semaphore_wait(barrier, 2 + videos - 1)

    def hop(step, piece, rightward):
        origin = ring_at((pos + n - step) % n if rightward else (pos + step) % n, n)
        sems = (send_r, recv_r) if rightward else (send_l, recv_l)
        return pltpu.make_async_remote_copy(
            src_ref=frames.at[origin, piece],
            dst_ref=frames.at[origin, piece],
            send_sem=sems[0].at[step, piece],
            recv_sem=sems[1].at[step, piece],
            device_id={"tm": right if rightward else left},
            device_id_type=MESH,
        )

    def every(count, body):
        def step(i, carry):
            body(i)
            return carry

        lax.fori_loop(0, count, step, 0)

    def first_hops(g):
        hop(0, g, True).start()
        hop(0, g, False).start()

    every(groups, first_hops)

    for copy in locals_[2:7]:
        copy.wait()
    wk = (wk_ref[...].astype(jnp.float32) * scale).astype(jnp.bfloat16)
    wk2[...] = jnp.concatenate([wk, wk], axis=0)
    wv2[...] = jnp.concatenate([wv_ref[...], wv_ref[...]], axis=0)
    pos_ref[...] = jnp.concatenate([tpos_ref[...], tpos_ref[...]], axis=1)
    top_ref[...] = jnp.full_like(top_ref, LOW)
    sum_ref[...] = jnp.zeros_like(sum_ref)
    acc_ref[...] = jnp.zeros_like(acc_ref)
    outer_ref[...] = jnp.zeros_like(outer_ref)
    locals_[1].wait()

    def keys_of(x):
        return jnp.dot(x, wk2[...], preferred_element_type=jnp.float32).astype(jnp.bfloat16)

    def wide_max(s):
        return jnp.broadcast_to(jnp.max(s, axis=1, keepdims=True), (s.shape[0], LANES))

    def recent(distance, g):
        origins = [ring_at((pos + n - distance) % n, n)]
        if distance < far:
            origins.append(ring_at((pos + distance) % n, n))
        xs, bias = [], []
        for origin in origins:
            offset = me - origin
            live = (offset >= 1) & (offset <= BACK)
            row = pos_ref[pl.ds(jnp.clip(offset - 1, 0, BACK - 1), 1), :]
            xs.append(split_tokens(frames[origin, g], row[None]))
            bias.append(jnp.full((1, TT), jnp.where(live, 0.0, LOW), jnp.float32))
        x = jnp.concatenate(xs, axis=1)
        width = x.shape[1]
        bias = jnp.concatenate(bias, axis=1)
        keys = keys_of(x.reshape(CLASSES * width, 2 * MD))
        s = jnp.concatenate(
            [
                lax.dot_general(
                    q_ref[g, c],
                    keys[c * width : (c + 1) * width],
                    DIMS_T,
                    preferred_element_type=jnp.float32,
                )
                for c in range(CLASSES)
            ],
            axis=0,
        )
        s = s + bias
        old = top_ref[g].reshape(CLASSES * TT, LANES)
        top = jnp.maximum(old, wide_max(s))
        p = jnp.exp(s - top[:, :width])
        fade = jnp.exp(old - top)
        part = p if width == LANES else jnp.concatenate([p, jnp.zeros_like(p)], axis=1)
        total = sum_ref[g].reshape(CLASSES * TT, LANES) * fade + part
        p = p.astype(jnp.bfloat16)
        u = jnp.concatenate(
            [
                jnp.dot(p[c * TT : (c + 1) * TT], x[c], preferred_element_type=jnp.float32)
                for c in range(CLASSES)
            ],
            axis=0,
        )
        acc = acc_ref[g].reshape(CLASSES * TT, 2 * MD) * fade + u
        top_ref[g] = top.reshape(CLASSES, TT, LANES)
        sum_ref[g] = total.reshape(CLASSES, TT, LANES)
        acc_ref[g] = acc.reshape(CLASSES, TT, 2 * MD)

    for distance in range(1, far):

        def arrive(g, distance=distance):
            for rightward in (True, False):
                hop(distance - 1, g, rightward).wait_recv()
                if distance < far - 1:
                    hop(distance, g, rightward).start()
            if distance == far - 1:
                @pl.when(g < half)
                def _():
                    hop(distance, g, True).start()

                @pl.when(g >= half)
                def _():
                    hop(distance, g, False).start()

            recent(distance, g)

        every(groups, arrive)

    def last(i):
        hop(far - 1, i, True).wait_recv()
        hop(far - 1, half + i, False).wait_recv()
        recent(far, i)
        recent(far, half + i)

    for i in range(half):
        last(i)
    locals_[7].wait()

    def finish(cls, carry):
        top = top_ref[:, cls].reshape(groups * TT, LANES)
        picked = []
        for s in range(entries):
            k = keyed_ref[cls + CLASSES * s]
            picked.append(frames[k // tiles, (k % tiles) // CLASSES, k % CLASSES])
        xk = split_tokens(jnp.concatenate(picked, axis=0), pos_ref[BACK : BACK + 1, :])
        q = q_ref[:, cls].reshape(groups * TT, d)
        sk = lax.dot_general(q, keys_of(xk), DIMS_T, preferred_element_type=jnp.float32)
        slabs = [sk[:, i : i + LANES] for i in range(0, sk.shape[1], LANES)]
        new = jnp.maximum(top, wide_max(functools.reduce(jnp.maximum, slabs)))
        pk = [jnp.exp(slab - new) for slab in slabs]
        fade = jnp.exp(top - new)
        total = sum_ref[:, cls].reshape(groups * TT, LANES)
        total = jnp.sum(total * fade + functools.reduce(jnp.add, pk), axis=1, keepdims=True)
        u = acc_ref[:, cls].reshape(groups * TT, 2 * MD) * fade + jnp.dot(
            jnp.concatenate([p.astype(jnp.bfloat16) for p in pk], axis=1),
            xk,
            preferred_element_type=jnp.float32,
        )
        u = (u / total).astype(jnp.bfloat16)
        mean_ref[cls] = u
        outer_ref[...] += lax.dot_general(
            u,
            cot_ref[:, cls].reshape(groups * TT, d),
            (((0,), (0,)), ((), ())),
            preferred_element_type=jnp.float32,
        )
        return carry

    lax.fori_loop(0, CLASSES, finish, 0, unroll=CLASSES)

    def term(step):
        other = (me + step) % n
        return pltpu.make_async_remote_copy(
            src_ref=terms.at[other],
            dst_ref=parts.at[step - 1],
            send_sem=send_a.at[step - 1],
            recv_sem=recv_a.at[step - 1],
            device_id={"tm": other},
            device_id_type=MESH,
        )

    def share_of(step):
        other = (vid + step) % videos
        return pltpu.make_async_remote_copy(
            src_ref=mine,
            dst_ref=sums.at[vid],
            send_sem=send_b.at[step - 1],
            recv_sem=recv_b.at[step - 1],
            device_id={"video": other},
            device_id_type=MESH,
        )

    outer = outer_ref[:MD] + outer_ref[MD:]
    high = outer.astype(jnp.bfloat16)
    low = (outer - high.astype(jnp.float32)).astype(jnp.bfloat16)
    grad_ref[...] = sum(
        lax.dot_general(
            wv_ref[...], half_, (((0,), (0,)), ((), ())), preferred_element_type=jnp.float32
        )
        for half_ in (high, low)
    )
    terms[...] = grad_ref[...].astype(jnp.bfloat16).reshape(terms.shape)
    for step in range(1, n):
        term(step).start()

    def project(cls, carry):
        attended = jnp.dot(mean_ref[cls], wv2[...], preferred_element_type=jnp.float32)
        out = jnp.dot(
            attended.astype(jnp.bfloat16), wo_ref[...], preferred_element_type=jnp.float32
        )
        branch_out[:, cls] = out.astype(jnp.bfloat16).reshape(groups, TT, d)
        return carry

    lax.fori_loop(0, CLASSES, project, 0)

    total = grad_ref[pl.ds(pl.multiple_of(me * rows, 8), rows), :]
    for step in range(1, n):
        term(step).wait_recv()
        total = total + parts[step - 1].astype(jnp.float32)
    mine[...] = total
    for step in range(1, videos):
        share_of(step).start()
    sums[vid] = total
    for step in range(1, videos):
        share_of(step).wait_recv()
    result = sums[0]
    for other in range(1, videos):
        result = result + sums[other]
    grad_out[...] = result * norm

    for step in range(far - 1):

        def sent(g, step=step):
            hop(step, g, True).wait_send()
            hop(step, g, False).wait_send()

        every(groups, sent)

    def last_sent(i):
        hop(far - 1, i, True).wait_send()
        hop(far - 1, half + i, False).wait_send()

    every(half, last_sent)
    for step in range(1, n):
        term(step).wait_send()
    for step in range(1, videos):
        share_of(step).wait_send()


def per_device(n, videos, queries, memory, tpos, w_k, w_v, w_o, keyframes, cot):
    tiles = memory.shape[2]
    d = queries.shape[-1]
    groups = tiles // CLASSES
    grouped = (groups, CLASSES, TT, d)
    packed = (TT // 2, 2 * MD)
    own = jnp.swapaxes(memory[0, 0].reshape((groups, CLASSES) + packed), 1, 2)
    rows = d // n
    vmem = pl.BlockSpec(memory_space=pltpu.VMEM)
    hbm = pl.BlockSpec(memory_space=pl.ANY)
    dma = pltpu.SemaphoreType.DMA
    f32, bf16 = jnp.float32, jnp.bfloat16
    hops = dma((n // 2, groups))
    norm = 1.0 / math.sqrt(videos * n * tiles * TT)
    branch, grad = pl.pallas_call(
        functools.partial(kernel, n, videos, norm),
        out_shape=(
            pltpu.VMEM(grouped, bf16),
            pltpu.VMEM((rows, d), f32),
        ),
        in_specs=[
            hbm, hbm, hbm, hbm, hbm, hbm, hbm, hbm,
        ],
        out_specs=(vmem, vmem),
        scratch_shapes=[
            pltpu.VMEM((n, groups, CLASSES) + packed, bf16),
            pltpu.SMEM(keyframes.shape[2:], jnp.int32),
            pltpu.VMEM(tpos.shape, f32),
            pltpu.VMEM(w_k.shape, bf16),
            pltpu.VMEM(w_v.shape, bf16),
            pltpu.VMEM(w_o.shape, bf16),
            pltpu.VMEM(own.shape, bf16),
            pltpu.VMEM(grouped, bf16),
            pltpu.VMEM(grouped, bf16),
            pltpu.VMEM((groups, CLASSES, TT, LANES), f32),
            pltpu.VMEM((groups, CLASSES, TT, LANES), f32),
            pltpu.VMEM((groups, CLASSES, TT, 2 * MD), f32),
            pltpu.VMEM((CLASSES, groups * TT, 2 * MD), bf16),
            pltpu.VMEM((2 * MD, d), bf16),
            pltpu.VMEM((2 * MD, d), bf16),
            pltpu.VMEM((BACK + 1, 2 * MD), f32),
            pltpu.VMEM((2 * MD, d), f32),
            pltpu.VMEM((d, d), f32),
            pltpu.VMEM((n, rows, d), bf16),
            pltpu.VMEM((n - 1, rows, d), bf16),
            pltpu.VMEM((rows, d), f32),
            pltpu.VMEM((videos, rows, d), f32),
            dma((8,)),
            hops, hops, hops, hops,
            dma((n - 1,)), dma((n - 1,)),
            dma((videos - 1,)), dma((videos - 1,)),
        ],
        compiler_params=pltpu.CompilerParams(
            collective_id=0, has_side_effects=True, vmem_limit_bytes=58 * 1024 * 1024
        ),
        name="attend",
    )(
        keyframes[0, 0], own, queries[0, 0].reshape(grouped), cot[0, 0].reshape(grouped),
        tpos, w_k, w_v, w_o,
    )
    return branch.reshape(queries.shape), grad


def solution(mesh):
    frame_spec = P("video", "tm", None, None)
    in_specs = (frame_spec, frame_spec, P(), P(), P(), P(), P("video", "tm", None), frame_spec)
    out_specs = (frame_spec, P("tm", None))
    return jax.shard_map(
        functools.partial(per_device, mesh.shape["tm"], mesh.shape["video"]),
        mesh=mesh,
        in_specs=in_specs,
        out_specs=out_specs,
        check_vma=False,
    )
```
